512 devices in a mesh: hrow: 16 (over y_lo, z), hcol: 32 (over x, y_hi, core).
Axes of the slice: x: 4, y: 8 (y_hi: 4, y_lo: 2; y = y_hi * 2 + y_lo), z: 8, core: 2. Of those that a mesh axis runs over, the one named last changes fastest.
Arguments:
- expect: bfloat16 [2, 1024, 102400], P(None, 'hrow', 'hcol'), may hold values from -6 to 6
- distrib: bfloat16 [2, 1024, 102400], P(None, 'hrow', 'hcol'), may hold values from -0.0024414062 to 0.0024414062
- direct: float32 [2, 2, 1024], P(None, None, 'hcol'), may hold values from -4 to 4
- pair_index: int32 [4, 2], replicated, may hold values from 0 to 1
Outputs:
- jacobian: float32 [4, 1024, 1024], P(None, 'hrow', 'hcol')
The draws below stay inside these ranges and needn't reach their ends.
Inputs may be any that keep to these rules, and one draw needn't show every extreme that they name: `pair_index`: column 0 of each row names a shock and column 1 an output; pairs may repeat.
All inputs are finite; a program needn't handle non-finite values.
Results may differ from the reference program's by a relative error of at most 0.0003.
Values may be sent and summed in bfloat16 or wider, within the bound.
A program may use at most 64 MiB of HBM per device.

```python
import jax
import jax.numpy as jnp
from jax import lax

SHOCKS = 2
OUTPUTS = 2
PAIRS = 4
HORIZON = 1024
GRID = 102400


def set_ends(values, key, smallest, largest):
    spot = [jax.random.randint(jax.random.fold_in(key, axis), (), 0, length) for axis, length in enumerate(values.shape)]
    main_axis = values.shape.index(max(values.shape))
    beside = spot[:main_axis] + [(spot[main_axis] + 1) % values.shape[main_axis]] + spot[main_axis + 1:]
    return values.at[tuple(spot)].set(smallest).at[tuple(beside)].set(largest)


def steps_of(own_key, extent, cuts, least, top_value):
    def one(position, blocks):
        draws = jax.random.uniform(jax.random.fold_in(jax.random.fold_in(own_key, 6), position), (blocks,), jnp.float32, least / len(cuts), top_value / len(cuts))
        return jnp.repeat(jnp.exp(draws), extent[position] // blocks).reshape((-1,) + (1,) * (len(extent) - position - 1))

    loudness = one(*cuts[0])
    for cut in cuts[1:]:
        loudness = loudness * one(*cut)
    return loudness


def noise(rng, dims, spread, bound, split=(), dtype=jnp.bfloat16):
    entries = spread * jax.random.normal(rng, dims, jnp.float32)
    if split:
        entries = entries * steps_of(rng, dims, split, -0.22, 0.18)
    return jnp.clip(entries, -bound, bound).astype(dtype)


def setup_inputs(seed: int = 0) -> dict:
    keys = jax.random.split(jax.random.key(seed), 5)
    expect = noise(keys[0], (OUTPUTS, HORIZON, GRID), 1.0, 6.0, ((1, 16), (2, 32)))
    distrib = noise(keys[1], (SHOCKS, HORIZON, GRID), (64 * GRID) ** -0.5, 0.0024414062, ((1, 16), (2, 32)))
    direct = noise(keys[2], (SHOCKS, OUTPUTS, HORIZON), 0.5, 4.0, ((2, 32),), jnp.float32)
    pair_index = set_ends(jax.random.randint(keys[3], (PAIRS, 2), 0, SHOCKS), jax.random.fold_in(keys[3], 1), 0, SHOCKS - 1).astype(jnp.int32)
    return dict(expect=expect, distrib=distrib, direct=direct, pair_index=pair_index)


def reference(expect, distrib, direct, pair_index):
    results = []
    for which in range(PAIRS):
        shock_id = pair_index[which, 0]
        output_id = pair_index[which, 1]
        outcome = jnp.take(expect, output_id, axis=0)
        response = jnp.take(distrib, shock_id, axis=0)
        fake_news = jnp.dot(outcome, response.T, preferred_element_type=jnp.float32)
        first_row = jnp.take(jnp.take(direct, shock_id, axis=0), output_id, axis=0)
        fake_news = fake_news.at[0].add(first_row)

        def advance(previous, current):
            moved_prev = jnp.concatenate([jnp.zeros((1,), jnp.float32), previous[:-1]])
            summed = current + moved_prev
            return summed, summed

        _, jacob_pair = lax.scan(advance, jnp.zeros((HORIZON,), jnp.float32), fake_news)
        results.append(jacob_pair)
    return jnp.stack(results)
```

```python
import functools

import jax
import jax.numpy as jnp
from jax import lax
from jax.experimental import pallas as pl
from jax.experimental.pallas import tpu as pltpu
from jax.sharding import PartitionSpec as P

PAIR = 2
RING = 8
COLS_X = 4
COLS_Y = 4
CORES = 2
ROWS = PAIR * RING
SPOTS = COLS_X * COLS_Y
MESH = pl.DeviceIdType.MESH


def kernel(
    e_hbm,
    d_hbm,
    direct_ref,
    out_ref,
    e_all,
    d_all,
    c_buf,
    x_buf,
    p_buf,
    slots,
    ends,
    carry,
    pad_direct,
    all_direct,
    swap_out,
    swap_in,
    local_sem,
    e_send,
    e_recv,
    d_send,
    d_recv,
    c_send,
    c_recv,
    p_send,
    p_recv,
    n_send,
    n_recv,
    s_send,
    s_recv,
):
    row = lax.axis_index("hrow")
    col = lax.axis_index("hcol")
    half = row // RING
    ring = row % RING
    core = col % CORES
    spot = col // CORES
    span = d_hbm.shape[0]
    dates = span // 2

    def ring_id(step):
        return (half * RING + lax.rem(ring + step + RING, RING), col)

    right, left = ring_id(1), ring_id(-1)
    mate = ((1 - half) * RING + ring, col)
    twin = (row, spot * CORES + (1 - core))

    def owner(block, band_half):
        return (band_half * RING + ring, (half * RING + block) * CORES + core)

    def signal(target):
        pl.semaphore_signal(barrier, inc=1, device_id=target, device_id_type=MESH)

    carry[...] = jnp.zeros_like(carry)
    pad_direct[...] = jnp.zeros_like(pad_direct)

    barrier = pltpu.get_barrier_semaphore()
    for target in (right, left, mate, twin):
        signal(target)
    source_half = spot // RING

    def greet_source(index, count):
        same = jnp.logical_and(source_half == half, index == spot)

        @pl.when(jnp.logical_not(same))
        def _():
            signal((source_half * RING + ring, index * CORES + core))

        return count + jnp.where(same, 0, 1)

    expected = lax.fori_loop(0, SPOTS, greet_source, jnp.int32(4))

    def link(down, side, way):
        other_row = row + way * down
        other_spot = spot + way * (down + side)
        valid = jnp.logical_and(other_row >= 0, other_row < ROWS)
        valid = jnp.logical_and(valid, jnp.logical_and(other_spot >= 0, other_spot < SPOTS))
        if side < 1:
            valid = jnp.logical_and(valid, down > 0)
        return valid, (other_row, other_spot * CORES + core)

    def greet_diagonal(down, count):
        for side in (-1, 0, 1):
            valid, upstream = link(down, side, -1)

            @pl.when(valid)
            def _():
                signal(upstream)

            valid, _ = link(down, side, 1)
            count = count + jnp.where(valid, 1, 0)
        return count

    expected = lax.fori_loop(0, ROWS, greet_diagonal, expected)

    own_e = pltpu.make_async_copy(e_hbm, e_all.at[half], local_sem.at[0])
    own_d = pltpu.make_async_copy(d_hbm, d_all.at[ring], local_sem.at[1])
    own_e.start()
    own_d.start()

    pl.semaphore_wait(barrier, expected)

    part = span // 4

    def piece(block, index):
        return d_all.at[block, pl.ds(index * part, part)]

    def d_copy(way, step, index, own):
        block = lax.rem(ring + (step if way else -step) + RING, RING)
        src = d_hbm.at[pl.ds(index * part, part)] if own else piece(block, index)
        return pltpu.make_async_remote_copy(
            src_ref=src,
            dst_ref=piece(block, index),
            send_sem=d_send.at[way, step, index],
            recv_sem=d_recv.at[way, step, index],
            device_id=left if way else right,
            device_id_type=MESH,
        )

    def d_arrival(way, step, index):
        block = lax.rem(ring + (step + 1 if way else -step - 1) + RING, RING)
        return pltpu.make_async_remote_copy(
            src_ref=piece(block, index),
            dst_ref=piece(block, index),
            send_sem=d_send.at[way, step, index],
            recv_sem=d_recv.at[way, step, index],
            device_id=left if way else right,
            device_id_type=MESH,
        )

    for index in range(4):
        for way in range(2):
            d_copy(way, 0, index, True).start()
    e_copy = pltpu.make_async_remote_copy(
        src_ref=e_hbm,
        dst_ref=e_all.at[half],
        send_sem=e_send,
        recv_sem=e_recv,
        device_id=mate,
        device_id_type=MESH,
    )
    e_copy.start()

    for shock in range(2):
        for outp in range(2):
            pad_direct[outp : outp + 1, shock * 64 : shock * 64 + 32] = direct_ref[shock, outp : outp + 1, :]
    own_direct = pad_direct[...]
    all_direct[0] = jnp.where(core == 0, own_direct, pltpu.roll(own_direct, 32, 1))
    direct_copy = pltpu.make_async_remote_copy(
        src_ref=all_direct.at[0],
        dst_ref=all_direct.at[1],
        send_sem=s_send.at[0],
        recv_sem=s_recv.at[0],
        device_id=twin,
        device_id_type=MESH,
    )
    direct_copy.start()

    def swap(turn):
        return pltpu.make_async_remote_copy(
            src_ref=c_buf.at[turn, :, 1 - core],
            dst_ref=x_buf.at[turn],
            send_sem=c_send.at[turn],
            recv_sem=c_recv.at[turn],
            device_id=twin,
            device_id_type=MESH,
        )

    def multiply(block, turn):
        product = lax.dot_general(
            e_all[...].reshape(2 * span, e_all.shape[2]),
            d_all[block],
            (((1,), (1,)), ((), ())),
            preferred_element_type=jnp.float32,
        )
        c_buf[turn] = product.reshape(2, 2, dates, span)
        swap(turn).start()

    def hand_over(block, band_half, turn):
        return pltpu.make_async_remote_copy(
            src_ref=p_buf.at[turn, band_half],
            dst_ref=slots.at[spot],
            send_sem=p_send.at[turn, band_half],
            recv_sem=p_recv.at[spot],
            device_id=owner(block, band_half),
            device_id_type=MESH,
        )

    def to_self(block, band_half):
        return jnp.logical_and(band_half == half, half * RING + block == spot)

    def deliver(block, turn):
        swap(turn).wait_recv()
        p_buf[turn] = c_buf[turn, :, core] + x_buf[turn]
        for band_half in range(2):
            mine = to_self(block, band_half)

            @pl.when(mine)
            def _():
                pltpu.make_async_copy(p_buf.at[turn, band_half], slots.at[spot], p_recv.at[spot]).start()

            @pl.when(jnp.logical_not(mine))
            def _():
                hand_over(block, band_half, turn).start()

    own_e.wait()
    own_d.wait()
    e_copy.wait_recv()
    multiply(ring, 0)
    deliver(ring, 0)

    def step_body(step, _):
        for index in range(4):
            for way in range(2):
                d_arrival(way, step - 1, index).wait_recv()
                if index // 2 == way:
                    d_copy(way, step, index, False).start()
                else:

                    @pl.when(step < 3)
                    def _():
                        d_copy(way, step, index, False).start()

        behind = lax.rem(ring - step + RING, RING)
        ahead = lax.rem(ring + step, RING)
        multiply(behind, 2 * step - 1)
        multiply(ahead, 2 * step)
        deliver(behind, 2 * step - 1)
        deliver(ahead, 2 * step)
        return 0

    lax.fori_loop(1, 4, step_body, 0)
    far = lax.rem(ring + 4, RING)
    for index in range(4):
        d_arrival(index // 2, 3, index).wait_recv()
    multiply(far, 7)
    deliver(far, 7)

    def arrived(index, _):
        pltpu.make_async_copy(slots.at[index], slots.at[index], p_recv.at[index]).wait()
        return 0

    lax.fori_loop(0, SPOTS, arrived, 0)
    total = slots[0]
    for index in range(1, SPOTS):
        total = total + slots[index]

    direct_copy.wait_recv()
    both_direct = all_direct[0] + all_direct[1]
    top = jnp.where(core == 0, both_direct[0:1], both_direct[1:2])
    top = jnp.where(row == 0, top, jnp.zeros_like(top))
    times = lax.broadcasted_iota(jnp.int32, (dates, span), 0)
    lanes = lax.broadcasted_iota(jnp.int32, (dates, span), 1)
    total = total + jnp.where(times == 0, top, 0.0)

    skewed = []
    for shock in range(2):
        tile = total if shock == 0 else pltpu.roll(total, 64, 1)
        tile = jnp.where(lanes < 64, tile, 0.0)
        for bit in range(6):
            moved = pltpu.roll(tile, 1 << bit, 1)
            tile = jnp.where(((63 - times) >> bit) & 1 == 1, moved, tile)
        skewed.append(tile)
        ends[shock : shock + 1, :] = jnp.sum(tile, axis=0, keepdims=True)

    def end_copy(down, side):
        valid, target = link(down, side, 1)
        return valid, pltpu.make_async_remote_copy(
            src_ref=ends,
            dst_ref=carry.at[down, side + 1],
            send_sem=n_send.at[down, side + 1],
            recv_sem=n_recv.at[down, side + 1],
            device_id=target,
            device_id_type=MESH,
        )

    def send_ends(down, _):
        for side in (-1, 0, 1):
            valid, copy = end_copy(down, side)

            @pl.when(valid)
            def _():
                copy.start()

        return 0

    lax.fori_loop(0, ROWS, send_ends, 0)

    summed = []
    for tile in skewed:
        for bit in range(6):
            offset = 1 << bit
            moved = pltpu.roll(tile, offset, 0)
            tile = tile + jnp.where(times >= offset, moved, 0.0)
        summed.append(tile)

    def receive_ends(down, _):
        for side in (-1, 0, 1):
            valid, _u = link(down, side, -1)

            @pl.when(valid)
            def _():
                end_copy(down, side)[1].wait_recv()

        return 0

    lax.fori_loop(0, ROWS, receive_ends, 0)
    incoming = jnp.sum(carry[...], axis=0)
    lane_row = lax.broadcasted_iota(jnp.int32, (2, span), 1)
    before = incoming[1]
    before = before + jnp.where(lane_row < 64, pltpu.roll(incoming[2], 64, 1), 0.0)
    before = before + jnp.where(lane_row >= 64, pltpu.roll(incoming[0], 64, 1), 0.0)

    finished = []
    for shock in range(2):
        tile = summed[shock] + before[shock : shock + 1]
        for bit in range(6):
            moved = pltpu.roll(tile, span - (1 << bit), 1)
            tile = jnp.where(((63 - times) >> bit) & 1 == 1, moved, tile)
        finished.append(tile)

    lower = finished
    upper = [pltpu.roll(tile, span - 32, 1) for tile in finished]
    mine = [jnp.where(core == 0, a, b) for a, b in zip(lower, upper)]
    theirs = [jnp.where(core == 0, b, a) for a, b in zip(lower, upper)]
    swap_out[...] = jnp.where(lanes < 32, theirs[0], pltpu.roll(theirs[1], 32, 1))
    last = pltpu.make_async_remote_copy(
        src_ref=swap_out,
        dst_ref=swap_in,
        send_sem=s_send.at[1],
        recv_sem=s_recv.at[1],
        device_id=twin,
        device_id_type=MESH,
    )
    last.start()
    for shock in range(2):
        out_ref[core, shock] = mine[shock][:, :32]

    def left_d(step, _):
        for index in range(4):
            for way in range(2):
                if index // 2 == way:
                    d_copy(way, step, index, False).wait_send()
                else:

                    @pl.when(step < 3)
                    def _():
                        d_copy(way, step, index, False).wait_send()

        return 0

    lax.fori_loop(0, 4, left_d, 0)
    e_copy.wait_send()
    direct_copy.wait_send()

    def left_p(turn, _):
        swap(turn).wait_send()
        away = (turn + 1) // 2
        block = lax.rem(ring + jnp.where(turn % 2 == 1, -away, away) + RING, RING)
        for band_half in range(2):

            @pl.when(jnp.logical_not(to_self(block, band_half)))
            def _():
                hand_over(block, band_half, turn).wait_send()

        return 0

    lax.fori_loop(0, RING, left_p, 0)

    def left_n(down, _):
        for side in (-1, 0, 1):
            valid, copy = end_copy(down, side)

            @pl.when(valid)
            def _():
                copy.wait_send()

        return 0

    lax.fori_loop(0, ROWS, left_n, 0)
    last.wait()
    received = swap_in[...]
    out_ref[1 - core, 0] = received[:, :32]
    out_ref[1 - core, 1] = pltpu.roll(received, span - 32, 1)[:, :32]


def blocks(expect, distrib, direct):
    outs, dates, points = expect.shape
    span = outs * dates
    dma = pltpu.SemaphoreType.DMA
    return pl.pallas_call(
        kernel,
        out_shape=jax.ShapeDtypeStruct((2, 2, dates, dates // 2), jnp.float32),
        in_specs=[
            pl.BlockSpec(memory_space=pl.ANY),
            pl.BlockSpec(memory_space=pl.ANY),
            pl.BlockSpec(memory_space=pltpu.VMEM),
        ],
        out_specs=pl.BlockSpec(memory_space=pltpu.VMEM),
        scratch_shapes=[
            pltpu.VMEM((PAIR, span, points), jnp.bfloat16),
            pltpu.VMEM((RING, span, points), jnp.bfloat16),
            pltpu.VMEM((RING, PAIR, 2, dates, span), jnp.float32),
            pltpu.VMEM((RING, PAIR, dates, span), jnp.float32),
            pltpu.VMEM((RING, PAIR, dates, span), jnp.float32),
            pltpu.VMEM((SPOTS, dates, span), jnp.float32),
            pltpu.VMEM((2, span), jnp.float32),
            pltpu.VMEM((ROWS, 3, 2, span), jnp.float32),
            pltpu.VMEM((8, span), jnp.float32),
            pltpu.VMEM((2, 8, span), jnp.float32),
            pltpu.VMEM((dates, span), jnp.float32),
            pltpu.VMEM((dates, span), jnp.float32),
            dma((2,)),
            dma,
            dma,
            dma((2, 4, 4)),
            dma((2, 4, 4)),
            dma((RING,)),
            dma((RING,)),
            dma((RING, PAIR)),
            dma((SPOTS,)),
            dma((ROWS, 3)),
            dma((ROWS, 3)),
            dma((2,)),
            dma((2,)),
        ],
        compiler_params=pltpu.CompilerParams(
            collective_id=0, has_side_effects=True, vmem_limit_bytes=40 * 1024 * 1024
        ),
    )(expect.reshape(span, points), distrib.reshape(span, points), direct)


def shards(expect, distrib, direct, pair_index):
    products = blocks(expect, distrib, direct)
    shock = pair_index[:, 0][:, None, None]
    outp = pair_index[:, 1][:, None, None]
    first = jnp.where(shock == 0, products[0, 0], products[0, 1])
    second = jnp.where(shock == 0, products[1, 0], products[1, 1])
    return jnp.where(outp == 0, first, second)


def solution(mesh):
    placed = (P(None, "hrow", "hcol"), P(None, "hrow", "hcol"), P(None, None, "hcol"), P())
    return jax.shard_map(
        shards, mesh=mesh, in_specs=placed, out_specs=P(None, "hrow", "hcol"), check_vma=False
    )
```

```python
import jax
import jax.numpy as jnp
from jax import lax
from jax.experimental import pallas as pl
from jax.experimental.pallas import tpu as pltpu
from jax.sharding import PartitionSpec as P

PAIR = 2
RING = 8
COLS_X = 4
COLS_Y = 4
CORES = 2
ROWS = PAIR * RING
SPOTS = COLS_X * COLS_Y
MESH = pl.DeviceIdType.MESH


def kernel(
    e_hbm,
    d_hbm,
    direct_ref,
    out_ref,
    e_all,
    d_all,
    c_buf,
    x_buf,
    p_buf,
    slots,
    ends,
    carry,
    pad_direct,
    all_direct,
    swap_out,
    swap_in,
    local_sem,
    e_send,
    e_recv,
    d_send,
    d_recv,
    c_send,
    c_recv,
    p_send,
    p_recv,
    n_send,
    n_recv,
    s_send,
    s_recv,
    word_sem,
):
    row = lax.axis_index("hrow")
    col = lax.axis_index("hcol")
    half = row // RING
    ring = row % RING
    core = col % CORES
    spot = col // CORES
    span = d_hbm.shape[0]
    dates = span // 2

    def ring_id(step):
        return (half * RING + lax.rem(ring + step + RING, RING), col)

    right, left = ring_id(1), ring_id(-1)
    mate = ((1 - half) * RING + ring, col)
    twin = (row, spot * CORES + (1 - core))

    def x_peer(step):
        return (row, lax.rem(spot + COLS_Y * step, SPOTS) * CORES + core)

    def y_peer(step):
        return (row, (spot // COLS_Y * COLS_Y + lax.rem(spot + step, COLS_Y)) * CORES + core)

    def owner(block, band_half):
        return (band_half * RING + ring, (half * RING + block) * CORES + core)

    def signal(target):
        pl.semaphore_signal(barrier, inc=1, device_id=target, device_id_type=MESH)

    carry[...] = jnp.zeros_like(carry)
    pad_direct[...] = jnp.zeros_like(pad_direct)

    barrier = pltpu.get_barrier_semaphore()
    for target in (right, left, mate, twin):
        signal(target)
    for step in (1, 2, 3):
        signal(x_peer(step))
        signal(y_peer(step))
    source_half = spot // RING

    def greet_source(index, count):
        same = jnp.logical_and(source_half == half, index == spot)

        @pl.when(jnp.logical_not(same))
        def _():
            signal((source_half * RING + ring, index * CORES + core))

        return count + jnp.where(same, 0, 1)

    expected = lax.fori_loop(0, SPOTS, greet_source, jnp.int32(10))

    def link(down, side, way):
        other_row = row + way * down
        other_spot = spot + way * (down + side)
        valid = jnp.logical_and(other_row >= 0, other_row < ROWS)
        valid = jnp.logical_and(valid, jnp.logical_and(other_spot >= 0, other_spot < SPOTS))
        if side < 1:
            valid = jnp.logical_and(valid, down > 0)
        return valid, (other_row, other_spot * CORES + core)

    own_e = pltpu.make_async_copy(e_hbm, e_all.at[half], local_sem.at[0])
    own_d = pltpu.make_async_copy(d_hbm, d_all.at[ring], local_sem.at[1])
    own_e.start()
    own_d.start()

    pl.semaphore_wait(barrier, expected)

    part = span // 4

    def piece(block, index):
        return d_all.at[block, pl.ds(index * part, part)]

    def d_copy(way, step, index, own):
        block = lax.rem(ring + (step if way else -step) + RING, RING)
        src = d_hbm.at[pl.ds(index * part, part)] if own else piece(block, index)
        return pltpu.make_async_remote_copy(
            src_ref=src,
            dst_ref=piece(block, index),
            send_sem=d_send.at[way, step, index],
            recv_sem=d_recv.at[way, step, index],
            device_id=left if way else right,
            device_id_type=MESH,
        )

    def d_arrival(way, step, index):
        block = lax.rem(ring + (step + 1 if way else -step - 1) + RING, RING)
        return pltpu.make_async_remote_copy(
            src_ref=piece(block, index),
            dst_ref=piece(block, index),
            send_sem=d_send.at[way, step, index],
            recv_sem=d_recv.at[way, step, index],
            device_id=left if way else right,
            device_id_type=MESH,
        )

    for index in range(4):
        for way in range(2):
            d_copy(way, 0, index, True).start()
    e_copy = pltpu.make_async_remote_copy(
        src_ref=e_hbm,
        dst_ref=e_all.at[half],
        send_sem=e_send,
        recv_sem=e_recv,
        device_id=mate,
        device_id_type=MESH,
    )
    e_copy.start()

    for shock in range(2):
        for outp in range(2):
            pad_direct[outp : outp + 1, shock * 64 : shock * 64 + 32] = direct_ref[shock, outp : outp + 1, :]
    own_direct = pad_direct[...]
    all_direct[0] = jnp.where(core == 0, own_direct, pltpu.roll(own_direct, 32, 1))
    direct_copy = pltpu.make_async_remote_copy(
        src_ref=all_direct.at[0],
        dst_ref=all_direct.at[1],
        send_sem=s_send.at[0],
        recv_sem=s_recv.at[0],
        device_id=twin,
        device_id_type=MESH,
    )
    direct_copy.start()

    def swap(turn):
        return pltpu.make_async_remote_copy(
            src_ref=c_buf.at[turn, :, 1 - core],
            dst_ref=x_buf.at[turn],
            send_sem=c_send.at[turn],
            recv_sem=c_recv.at[turn],
            device_id=twin,
            device_id_type=MESH,
        )

    def multiply(block, turn):
        product = lax.dot_general(
            e_all[...].reshape(2 * span, e_all.shape[2]),
            d_all[block],
            (((1,), (1,)), ((), ())),
            preferred_element_type=jnp.float32,
        )
        c_buf[turn] = product.reshape(2, 2, dates, span)
        swap(turn).start()

    def hand_over(block, band_half, turn):
        return pltpu.make_async_remote_copy(
            src_ref=p_buf.at[turn, band_half],
            dst_ref=slots.at[spot],
            send_sem=p_send.at[turn, band_half],
            recv_sem=p_recv.at[spot],
            device_id=owner(block, band_half),
            device_id_type=MESH,
        )

    def to_self(block, band_half):
        return jnp.logical_and(band_half == half, half * RING + block == spot)

    def deliver(block, turn):
        swap(turn).wait_recv()
        p_buf[turn] = c_buf[turn, :, core] + x_buf[turn]
        for band_half in range(2):
            mine = to_self(block, band_half)

            @pl.when(mine)
            def _():
                pltpu.make_async_copy(p_buf.at[turn, band_half], slots.at[spot], p_recv.at[spot]).start()

            @pl.when(jnp.logical_not(mine))
            def _():
                hand_over(block, band_half, turn).start()

    def step_body(step, _):
        for index in range(4):
            for way in range(2):
                d_arrival(way, step - 1, index).wait_recv()
                if index // 2 == way:
                    d_copy(way, step, index, False).start()
                else:

                    @pl.when(step < 3)
                    def _():
                        d_copy(way, step, index, False).start()

        @pl.when(step == 1)
        def _():
            own_e.wait()
            own_d.wait()
            e_copy.wait_recv()
            multiply(ring, 0)
            deliver(ring, 0)

        behind = lax.rem(ring - step + RING, RING)
        ahead = lax.rem(ring + step, RING)
        multiply(behind, 2 * step - 1)
        multiply(ahead, 2 * step)
        deliver(behind, 2 * step - 1)
        deliver(ahead, 2 * step)
        return 0

    lax.fori_loop(1, 4, step_body, 0)
    far = lax.rem(ring + 4, RING)
    for index in range(4):
        d_arrival(index // 2, 3, index).wait_recv()
    pl.semaphore_signal(word_sem.at[0], inc=1, device_id=mate, device_id_type=MESH)
    multiply(far, 7)
    pl.semaphore_wait(word_sem.at[0], 1)
    for step in (1, 2, 3):
        pl.semaphore_signal(word_sem.at[1], inc=1, device_id=x_peer(step), device_id_type=MESH)
    deliver(far, 7)
    pl.semaphore_wait(word_sem.at[1], 3)
    for step in (1, 2, 3):
        pl.semaphore_signal(word_sem.at[2], inc=1, device_id=y_peer(step), device_id_type=MESH)

    def arrived(index, _):
        pltpu.make_async_copy(slots.at[index], slots.at[index], p_recv.at[index]).wait()
        return 0

    lax.fori_loop(0, SPOTS, arrived, 0)
    total = slots[0]
    for index in range(1, SPOTS):
        total = total + slots[index]

    direct_copy.wait_recv()
    both_direct = all_direct[0] + all_direct[1]
    top = jnp.where(core == 0, both_direct[0:1], both_direct[1:2])
    top = jnp.where(row == 0, top, jnp.zeros_like(top))
    times = lax.broadcasted_iota(jnp.int32, (dates, span), 0)
    lanes = lax.broadcasted_iota(jnp.int32, (dates, span), 1)
    total = total + jnp.where(times == 0, top, 0.0)

    skewed = []
    for shock in range(2):
        tile = total if shock == 0 else pltpu.roll(total, 64, 1)
        tile = jnp.where(lanes < 64, tile, 0.0)
        for bit in range(6):
            moved = pltpu.roll(tile, 1 << bit, 1)
            tile = jnp.where(((63 - times) >> bit) & 1 == 1, moved, tile)
        skewed.append(tile)
        ends[shock : shock + 1, :] = jnp.sum(tile, axis=0, keepdims=True)

    def end_copy(down, side):
        valid, target = link(down, side, 1)
        return valid, pltpu.make_async_remote_copy(
            src_ref=ends,
            dst_ref=carry.at[down, side + 1],
            send_sem=n_send.at[down, side + 1],
            recv_sem=n_recv.at[down, side + 1],
            device_id=target,
            device_id_type=MESH,
        )

    def send_ends(down, _):
        for side in (-1, 0, 1):
            valid, copy = end_copy(down, side)

            @pl.when(valid)
            def _():
                copy.start()

        return 0

    pl.semaphore_wait(word_sem.at[2], 3)
    lax.fori_loop(0, ROWS, send_ends, 0)

    summed = []
    for tile in skewed:
        for bit in range(6):
            offset = 1 << bit
            moved = pltpu.roll(tile, offset, 0)
            tile = tile + jnp.where(times >= offset, moved, 0.0)
        summed.append(tile)

    def receive_ends(down, _):
        for side in (-1, 0, 1):
            valid, _u = link(down, side, -1)

            @pl.when(valid)
            def _():
                end_copy(down, side)[1].wait_recv()

        return 0

    lax.fori_loop(0, ROWS, receive_ends, 0)
    incoming = jnp.sum(carry[...], axis=0)
    lane_row = lax.broadcasted_iota(jnp.int32, (2, span), 1)
    before = incoming[1]
    before = before + jnp.where(lane_row < 64, pltpu.roll(incoming[2], 64, 1), 0.0)
    before = before + jnp.where(lane_row >= 64, pltpu.roll(incoming[0], 64, 1), 0.0)

    finished = []
    for shock in range(2):
        tile = summed[shock] + before[shock : shock + 1]
        for bit in range(6):
            moved = pltpu.roll(tile, span - (1 << bit), 1)
            tile = jnp.where(((63 - times) >> bit) & 1 == 1, moved, tile)
        finished.append(tile)

    lower = finished
    upper = [pltpu.roll(tile, span - 32, 1) for tile in finished]
    mine = [jnp.where(core == 0, a, b) for a, b in zip(lower, upper)]
    theirs = [jnp.where(core == 0, b, a) for a, b in zip(lower, upper)]
    swap_out[...] = jnp.where(lanes < 32, theirs[0], pltpu.roll(theirs[1], 32, 1))
    last = pltpu.make_async_remote_copy(
        src_ref=swap_out,
        dst_ref=swap_in,
        send_sem=s_send.at[1],
        recv_sem=s_recv.at[1],
        device_id=twin,
        device_id_type=MESH,
    )
    last.start()
    for shock in range(2):
        out_ref[core, shock] = mine[shock][:, :32]

    def left_d(step, _):
        for index in range(4):
            for way in range(2):
                if index // 2 == way:
                    d_copy(way, step, index, False).wait_send()
                else:

                    @pl.when(step < 3)
                    def _():
                        d_copy(way, step, index, False).wait_send()

        return 0

    lax.fori_loop(0, 4, left_d, 0)
    e_copy.wait_send()
    direct_copy.wait_send()

    def left_p(turn, _):
        swap(turn).wait_send()
        away = (turn + 1) // 2
        block = lax.rem(ring + jnp.where(turn % 2 == 1, -away, away) + RING, RING)
        for band_half in range(2):

            @pl.when(jnp.logical_not(to_self(block, band_half)))
            def _():
                hand_over(block, band_half, turn).wait_send()

        return 0

    lax.fori_loop(0, RING, left_p, 0)

    def left_n(down, _):
        for side in (-1, 0, 1):
            valid, copy = end_copy(down, side)

            @pl.when(valid)
            def _():
                copy.wait_send()

        return 0

    lax.fori_loop(0, ROWS, left_n, 0)
    last.wait()
    received = swap_in[...]
    out_ref[1 - core, 0] = received[:, :32]
    out_ref[1 - core, 1] = pltpu.roll(received, span - 32, 1)[:, :32]


def blocks(expect, distrib, direct):
    outs, dates, points = expect.shape
    span = outs * dates
    dma = pltpu.SemaphoreType.DMA
    return pl.pallas_call(
        kernel,
        out_shape=jax.ShapeDtypeStruct((2, 2, dates, dates // 2), jnp.float32),
        in_specs=[
            pl.BlockSpec(memory_space=pl.ANY),
            pl.BlockSpec(memory_space=pl.ANY),
            pl.BlockSpec(memory_space=pltpu.VMEM),
        ],
        out_specs=pl.BlockSpec(memory_space=pltpu.VMEM),
        scratch_shapes=[
            pltpu.VMEM((PAIR, span, points), jnp.bfloat16),
            pltpu.VMEM((RING, span, points), jnp.bfloat16),
            pltpu.VMEM((RING, PAIR, 2, dates, span), jnp.float32),
            pltpu.VMEM((RING, PAIR, dates, span), jnp.float32),
            pltpu.VMEM((RING, PAIR, dates, span), jnp.float32),
            pltpu.VMEM((SPOTS, dates, span), jnp.float32),
            pltpu.VMEM((2, span), jnp.float32),
            pltpu.VMEM((ROWS, 3, 2, span), jnp.float32),
            pltpu.VMEM((8, span), jnp.float32),
            pltpu.VMEM((2, 8, span), jnp.float32),
            pltpu.VMEM((dates, span), jnp.float32),
            pltpu.VMEM((dates, span), jnp.float32),
            dma((2,)),
            dma,
            dma,
            dma((2, 4, 4)),
            dma((2, 4, 4)),
            dma((RING,)),
            dma((RING,)),
            dma((RING, PAIR)),
            dma((SPOTS,)),
            dma((ROWS, 3)),
            dma((ROWS, 3)),
            dma((2,)),
            dma((2,)),
            pltpu.SemaphoreType.REGULAR((3,)),
        ],
        compiler_params=pltpu.CompilerParams(
            collective_id=0, has_side_effects=True, vmem_limit_bytes=58 * 1024 * 1024
        ),
    )(expect.reshape(span, points), distrib.reshape(span, points), direct)


def shards(expect, distrib, direct, pair_index):
    products = blocks(expect, distrib, direct)
    shock = pair_index[:, 0][:, None, None]
    outp = pair_index[:, 1][:, None, None]
    first = jnp.where(shock == 0, products[0, 0], products[0, 1])
    second = jnp.where(shock == 0, products[1, 0], products[1, 1])
    return jnp.where(outp == 0, first, second)


def solution(mesh):
    placed = (P(None, "hrow", "hcol"), P(None, "hrow", "hcol"), P(None, None, "hcol"), P())
    return jax.shard_map(
        shards, mesh=mesh, in_specs=placed, out_specs=P(None, "hrow", "hcol"), check_vma=False
    )
```

```python
import jax
import jax.numpy as jnp
from jax import lax
from jax.experimental import pallas as pl
from jax.experimental.pallas import tpu as pltpu
from jax.sharding import PartitionSpec as P

PAIR = 2
RING = 8
COLS_X = 4
COLS_Y = 4
CORES = 2
ROWS = PAIR * RING
SPOTS = COLS_X * COLS_Y
MESH = pl.DeviceIdType.MESH


def kernel(
    e_hbm,
    d_hbm,
    direct_hbm,
    out_ref,
    e_all,
    d_all,
    c_buf,
    x_buf,
    p_buf,
    slots,
    ends,
    carry,
    direct_ref,
    pad_direct,
    all_direct,
    swap_out,
    swap_in,
    local_sem,
    e_send,
    e_recv,
    d_send,
    d_recv,
    c_send,
    c_recv,
    p_send,
    p_recv,
    n_send,
    n_recv,
    s_send,
    s_recv,
    word_sem,
):
    row = lax.axis_index("hrow")
    col = lax.axis_index("hcol")
    half = row // RING
    ring = row % RING
    core = col % CORES
    spot = col // CORES
    span = d_hbm.shape[0]
    dates = span // 2

    def ring_id(step):
        return (half * RING + lax.rem(ring + step + RING, RING), col)

    right, left = ring_id(1), ring_id(-1)
    mate = ((1 - half) * RING + ring, col)
    twin = (row, spot * CORES + (1 - core))

    def x_peer(step):
        return (row, lax.rem(spot + COLS_Y * step, SPOTS) * CORES + core)

    def y_peer(step):
        return (row, (spot // COLS_Y * COLS_Y + lax.rem(spot + step, COLS_Y)) * CORES + core)

    def owner(block, band_half):
        return (band_half * RING + ring, (half * RING + block) * CORES + core)

    def signal(target):
        pl.semaphore_signal(barrier, inc=1, device_id=target, device_id_type=MESH)

    carry[...] = jnp.zeros_like(carry)
    pad_direct[...] = jnp.zeros_like(pad_direct)

    barrier = pltpu.get_barrier_semaphore()
    for target in (right, left, mate, twin):
        signal(target)
    for step in (1, 2, 3):
        signal(x_peer(step))
        signal(y_peer(step))
    source_half = spot // RING

    def greet_source(index, count):
        same = jnp.logical_and(source_half == half, index == spot)

        @pl.when(jnp.logical_not(same))
        def _():
            signal((source_half * RING + ring, index * CORES + core))

        return count + jnp.where(same, 0, 1)

    expected = lax.fori_loop(0, SPOTS, greet_source, jnp.int32(10))

    def link(down, side, way):
        other_row = row + way * down
        other_spot = spot + way * (down + side)
        valid = jnp.logical_and(other_row >= 0, other_row < ROWS)
        valid = jnp.logical_and(valid, jnp.logical_and(other_spot >= 0, other_spot < SPOTS))
        if side < 1:
            valid = jnp.logical_and(valid, down > 0)
        return valid, (other_row, other_spot * CORES + core)

    own_e = pltpu.make_async_copy(e_hbm, e_all.at[half], local_sem.at[0])
    own_d = pltpu.make_async_copy(d_hbm, d_all.at[ring], local_sem.at[1])
    own_direct = pltpu.make_async_copy(direct_hbm, direct_ref, local_sem.at[2])
    own_direct.start()
    own_e.start()
    own_d.start()

    pl.semaphore_wait(barrier, expected)

    part = span // 4

    def piece(block, index):
        return d_all.at[block, pl.ds(index * part, part)]

    def d_copy(way, step, index, own):
        block = lax.rem(ring + (step if way else -step) + RING, RING)
        src = d_hbm.at[pl.ds(index * part, part)] if own else piece(block, index)
        return pltpu.make_async_remote_copy(
            src_ref=src,
            dst_ref=piece(block, index),
            send_sem=d_send.at[way, step, index],
            recv_sem=d_recv.at[way, step, index],
            device_id=left if way else right,
            device_id_type=MESH,
        )

    def d_arrival(way, step, index):
        block = lax.rem(ring + (step + 1 if way else -step - 1) + RING, RING)
        return pltpu.make_async_remote_copy(
            src_ref=piece(block, index),
            dst_ref=piece(block, index),
            send_sem=d_send.at[way, step, index],
            recv_sem=d_recv.at[way, step, index],
            device_id=left if way else right,
            device_id_type=MESH,
        )

    for index in range(4):
        for way in range(2):
            d_copy(way, 0, index, True).start()
    e_copy = pltpu.make_async_remote_copy(
        src_ref=e_hbm,
        dst_ref=e_all.at[half],
        send_sem=e_send,
        recv_sem=e_recv,
        device_id=mate,
        device_id_type=MESH,
    )
    e_copy.start()

    own_direct.wait()
    for shock in range(2):
        for outp in range(2):
            pad_direct[outp : outp + 1, shock * 64 : shock * 64 + 32] = direct_ref[shock, outp : outp + 1, :]
    raw_direct = pad_direct[...]
    all_direct[0] = jnp.where(core == 0, raw_direct, pltpu.roll(raw_direct, 32, 1))
    direct_copy = pltpu.make_async_remote_copy(
        src_ref=all_direct.at[0],
        dst_ref=all_direct.at[1],
        send_sem=s_send.at[0],
        recv_sem=s_recv.at[0],
        device_id=twin,
        device_id_type=MESH,
    )
    direct_copy.start()

    def swap(turn):
        return pltpu.make_async_remote_copy(
            src_ref=c_buf.at[turn, :, 1 - core],
            dst_ref=x_buf.at[turn],
            send_sem=c_send.at[turn],
            recv_sem=c_recv.at[turn],
            device_id=twin,
            device_id_type=MESH,
        )

    def multiply(block, turn):
        product = lax.dot_general(
            e_all[...].reshape(2 * span, e_all.shape[2]),
            d_all[block],
            (((1,), (1,)), ((), ())),
            preferred_element_type=jnp.float32,
        )
        c_buf[turn] = product.reshape(2, 2, dates, span)
        swap(turn).start()

    def hand_over(block, band_half, turn):
        return pltpu.make_async_remote_copy(
            src_ref=p_buf.at[turn, band_half],
            dst_ref=slots.at[spot],
            send_sem=p_send.at[turn, band_half],
            recv_sem=p_recv.at[spot],
            device_id=owner(block, band_half),
            device_id_type=MESH,
        )

    def to_self(block, band_half):
        return jnp.logical_and(band_half == half, half * RING + block == spot)

    def deliver(block, turn):
        swap(turn).wait_recv()
        p_buf[turn] = c_buf[turn, :, core] + x_buf[turn]
        for band_half in range(2):
            mine = to_self(block, band_half)

            @pl.when(mine)
            def _():
                pltpu.make_async_copy(p_buf.at[turn, band_half], slots.at[spot], p_recv.at[spot]).start()

            @pl.when(jnp.logical_not(mine))
            def _():
                hand_over(block, band_half, turn).start()

    def pass_on(step):
        for index in range(4):
            for way in range(2):
                d_arrival(way, step - 1, index).wait_recv()
                if index // 2 == way:
                    d_copy(way, step, index, False).start()
                else:

                    @pl.when(step < 3)
                    def _():
                        d_copy(way, step, index, False).start()

    def block_at(turn):
        away = (turn + 1) // 2
        return lax.rem(ring + jnp.where(turn % 2 == 1, -away, away) + RING, RING)

    def turn_body(turn, _):
        opens_step = jnp.logical_or(turn == 0, jnp.logical_or(turn == 3, turn == 5))

        @pl.when(opens_step)
        def _():
            pass_on(jnp.where(turn == 0, 1, (turn + 1) // 2))

        @pl.when(turn == 0)
        def _():
            own_e.wait()
            own_d.wait()
            e_copy.wait_recv()

        @pl.when(turn == 7)
        def _():
            for index in range(4):
                d_arrival(index // 2, 3, index).wait_recv()
            pl.semaphore_signal(word_sem.at[0], inc=1, device_id=mate, device_id_type=MESH)

        multiply(block_at(turn), turn)

        @pl.when(turn == 7)
        def _():
            pl.semaphore_wait(word_sem.at[0], 1)
            for step in (1, 2, 3):
                pl.semaphore_signal(word_sem.at[1], inc=1, device_id=x_peer(step), device_id_type=MESH)

        @pl.when(jnp.logical_and(turn % 2 == 0, turn > 0))
        def _():
            deliver(block_at(turn - 1), turn - 1)

        @pl.when(jnp.logical_or(turn % 2 == 0, turn == 7))
        def _():
            deliver(block_at(turn), turn)

        return 0

    lax.fori_loop(0, RING, turn_body, 0)
    pl.semaphore_wait(word_sem.at[1], 3)
    for step in (1, 2, 3):
        pl.semaphore_signal(word_sem.at[2], inc=1, device_id=y_peer(step), device_id_type=MESH)

    def arrived(index, _):
        pltpu.make_async_copy(slots.at[index], slots.at[index], p_recv.at[index]).wait()
        return 0

    lax.fori_loop(0, SPOTS, arrived, 0)
    total = slots[0]
    for index in range(1, SPOTS):
        total = total + slots[index]

    direct_copy.wait_recv()
    both_direct = all_direct[0] + all_direct[1]
    top = jnp.where(core == 0, both_direct[0:1], both_direct[1:2])
    top = jnp.where(row == 0, top, jnp.zeros_like(top))
    times = lax.broadcasted_iota(jnp.int32, (dates, span), 0)
    lanes = lax.broadcasted_iota(jnp.int32, (dates, span), 1)
    total = total + jnp.where(times == 0, top, 0.0)

    skewed = []
    for shock in range(2):
        tile = total if shock == 0 else pltpu.roll(total, 64, 1)
        tile = jnp.where(lanes < 64, tile, 0.0)
        for bit in range(6):
            moved = pltpu.roll(tile, 1 << bit, 1)
            tile = jnp.where(((63 - times) >> bit) & 1 == 1, moved, tile)
        skewed.append(tile)
        ends[shock : shock + 1, :] = jnp.sum(tile, axis=0, keepdims=True)

    def end_copy(down, side):
        valid, target = link(down, side, 1)
        return valid, pltpu.make_async_remote_copy(
            src_ref=ends,
            dst_ref=carry.at[down, side + 1],
            send_sem=n_send.at[down, side + 1],
            recv_sem=n_recv.at[down, side + 1],
            device_id=target,
            device_id_type=MESH,
        )

    def send_ends(down, _):
        for side in (-1, 0, 1):
            valid, copy = end_copy(down, side)

            @pl.when(valid)
            def _():
                copy.start()

        return 0

    pl.semaphore_wait(word_sem.at[2], 3)
    lax.fori_loop(0, ROWS, send_ends, 0)

    summed = []
    for tile in skewed:
        for bit in range(6):
            offset = 1 << bit
            moved = pltpu.roll(tile, offset, 0)
            tile = tile + jnp.where(times >= offset, moved, 0.0)
        summed.append(tile)

    def left_d(step, _):
        for index in range(4):
            for way in range(2):
                if index // 2 == way:
                    d_copy(way, step, index, False).wait_send()
                else:

                    @pl.when(step < 3)
                    def _():
                        d_copy(way, step, index, False).wait_send()

        return 0

    lax.fori_loop(0, 4, left_d, 0)
    e_copy.wait_send()
    direct_copy.wait_send()

    def left_p(turn, _):
        swap(turn).wait_send()
        block = block_at(turn)
        for band_half in range(2):

            @pl.when(jnp.logical_not(to_self(block, band_half)))
            def _():
                hand_over(block, band_half, turn).wait_send()

        return 0

    lax.fori_loop(0, RING, left_p, 0)

    def receive_ends(down, _):
        for side in (-1, 0, 1):
            valid, _u = link(down, side, -1)

            @pl.when(valid)
            def _():
                end_copy(down, side)[1].wait_recv()

        return 0

    lax.fori_loop(0, ROWS, receive_ends, 0)
    incoming = jnp.sum(carry[...], axis=0)
    lane_row = lax.broadcasted_iota(jnp.int32, (2, span), 1)
    before = incoming[1]
    before = before + jnp.where(lane_row < 64, pltpu.roll(incoming[2], 64, 1), 0.0)
    before = before + jnp.where(lane_row >= 64, pltpu.roll(incoming[0], 64, 1), 0.0)

    finished = []
    for shock in range(2):
        tile = summed[shock] + before[shock : shock + 1]
        for bit in range(6):
            moved = pltpu.roll(tile, span - (1 << bit), 1)
            tile = jnp.where(((63 - times) >> bit) & 1 == 1, moved, tile)
        finished.append(tile)

    lower = finished
    upper = [pltpu.roll(tile, span - 32, 1) for tile in finished]
    mine = [jnp.where(core == 0, a, b) for a, b in zip(lower, upper)]
    theirs = [jnp.where(core == 0, b, a) for a, b in zip(lower, upper)]
    swap_out[...] = jnp.where(lanes < 32, theirs[0], pltpu.roll(theirs[1], 32, 1))
    last = pltpu.make_async_remote_copy(
        src_ref=swap_out,
        dst_ref=swap_in,
        send_sem=s_send.at[1],
        recv_sem=s_recv.at[1],
        device_id=twin,
        device_id_type=MESH,
    )
    last.start()
    for shock in range(2):
        out_ref[core, shock] = mine[shock][:, :32]

    def left_n(down, _):
        for side in (-1, 0, 1):
            valid, copy = end_copy(down, side)

            @pl.when(valid)
            def _():
                copy.wait_send()

        return 0

    lax.fori_loop(0, ROWS, left_n, 0)
    last.wait()
    received = swap_in[...]
    out_ref[1 - core, 0] = received[:, :32]
    out_ref[1 - core, 1] = pltpu.roll(received, span - 32, 1)[:, :32]


def blocks(expect, distrib, direct):
    outs, dates, points = expect.shape
    span = outs * dates
    dma = pltpu.SemaphoreType.DMA
    return pl.pallas_call(
        kernel,
        out_shape=jax.ShapeDtypeStruct((2, 2, dates, dates // 2), jnp.float32),
        in_specs=[
            pl.BlockSpec(memory_space=pl.ANY),
            pl.BlockSpec(memory_space=pl.ANY),
            pl.BlockSpec(memory_space=pl.ANY),
        ],
        out_specs=pl.BlockSpec(memory_space=pltpu.VMEM),
        scratch_shapes=[
            pltpu.VMEM((PAIR, span, points), jnp.bfloat16),
            pltpu.VMEM((RING, span, points), jnp.bfloat16),
            pltpu.VMEM((RING, PAIR, 2, dates, span), jnp.float32),
            pltpu.VMEM((RING, PAIR, dates, span), jnp.float32),
            pltpu.VMEM((RING, PAIR, dates, span), jnp.float32),
            pltpu.VMEM((SPOTS, dates, span), jnp.float32),
            pltpu.VMEM((2, span), jnp.float32),
            pltpu.VMEM((ROWS, 3, 2, span), jnp.float32),
            pltpu.VMEM((2, 2, dates // 2), jnp.float32),
            pltpu.VMEM((8, span), jnp.float32),
            pltpu.VMEM((2, 8, span), jnp.float32),
            pltpu.VMEM((dates, span), jnp.float32),
            pltpu.VMEM((dates, span), jnp.float32),
            dma((3,)),
            dma,
            dma,
            dma((2, 4, 4)),
            dma((2, 4, 4)),
            dma((RING,)),
            dma((RING,)),
            dma((RING, PAIR)),
            dma((SPOTS,)),
            dma((ROWS, 3)),
            dma((ROWS, 3)),
            dma((2,)),
            dma((2,)),
            pltpu.SemaphoreType.REGULAR((3,)),
        ],
        compiler_params=pltpu.CompilerParams(
            collective_id=0, has_side_effects=True, vmem_limit_bytes=58 * 1024 * 1024
        ),
    )(expect.reshape(span, points), distrib.reshape(span, points), direct)


def shards(expect, distrib, direct, pair_index):
    products = blocks(expect, distrib, direct)
    shock = pair_index[:, 0][:, None, None]
    outp = pair_index[:, 1][:, None, None]
    first = jnp.where(shock == 0, products[0, 0], products[0, 1])
    second = jnp.where(shock == 0, products[1, 0], products[1, 1])
    return jnp.where(outp == 0, first, second)


def solution(mesh):
    placed = (P(None, "hrow", "hcol"), P(None, "hrow", "hcol"), P(None, None, "hcol"), P())
    return jax.shard_map(
        shards, mesh=mesh, in_specs=placed, out_specs=P(None, "hrow", "hcol"), check_vma=False
    )
```

```python
import jax
import jax.numpy as jnp
from jax import lax
from jax.experimental import pallas as pl
from jax.experimental.pallas import tpu as pltpu
from jax.sharding import PartitionSpec as P

PAIR = 2
RING = 8
COLS_X = 4
COLS_Y = 4
CORES = 2
ROWS = PAIR * RING
SPOTS = COLS_X * COLS_Y
MESH = pl.DeviceIdType.MESH


def kernel(
    e_hbm,
    d_hbm,
    direct_hbm,
    out_ref,
    e_all,
    d_all,
    c_buf,
    x_buf,
    p_buf,
    slots,
    ends,
    carry,
    direct_ref,
    pad_direct,
    all_direct,
    swap_out,
    swap_in,
    local_sem,
    e_send,
    e_recv,
    d_send,
    d_recv,
    c_send,
    c_recv,
    p_send,
    p_recv,
    n_send,
    n_recv,
    s_send,
    s_recv,
    word_sem,
):
    row = lax.axis_index("hrow")
    col = lax.axis_index("hcol")
    half = row // RING
    ring = row % RING
    core = col % CORES
    spot = col // CORES
    span = d_hbm.shape[0]
    dates = span // 2

    def ring_id(step):
        return (half * RING + lax.rem(ring + step + RING, RING), col)

    right, left = ring_id(1), ring_id(-1)
    mate = ((1 - half) * RING + ring, col)
    twin = (row, spot * CORES + (1 - core))

    def x_peer(step):
        return (row, lax.rem(spot + COLS_Y * step, SPOTS) * CORES + core)

    def mate_x_peer(step):
        return (mate[0], x_peer(step)[1])

    def y_peer(step):
        return (row, (spot // COLS_Y * COLS_Y + lax.rem(spot + step, COLS_Y)) * CORES + core)

    def owner(block, band_half):
        return (band_half * RING + ring, (half * RING + block) * CORES + core)

    def signal(target):
        pl.semaphore_signal(barrier, inc=1, device_id=target, device_id_type=MESH)


    carry[...] = jnp.zeros_like(carry)
    pad_direct[...] = jnp.zeros_like(pad_direct)

    barrier = pltpu.get_barrier_semaphore()
    for target in (right, left, mate, twin):
        signal(target)
    for step in (1, 2, 3):
        signal(x_peer(step))
        signal(y_peer(step))
        signal(mate_x_peer(step))
    source_half = spot // RING

    def greet_source(index, count):
        same = jnp.logical_and(source_half == half, index == spot)

        @pl.when(jnp.logical_not(same))
        def _():
            signal((source_half * RING + ring, index * CORES + core))

        return count + jnp.where(same, 0, 1)

    expected = lax.fori_loop(0, SPOTS, greet_source, jnp.int32(13))

    def link(down, side, way):
        other_row = row + way * down
        other_spot = spot + way * (down + side)
        valid = jnp.logical_and(other_row >= 0, other_row < ROWS)
        valid = jnp.logical_and(valid, jnp.logical_and(other_spot >= 0, other_spot < SPOTS))
        if side < 1:
            valid = jnp.logical_and(valid, down > 0)
        return valid, (other_row, other_spot * CORES + core)

    own_e = pltpu.make_async_copy(e_hbm, e_all.at[half], local_sem.at[0])
    own_d = pltpu.make_async_copy(d_hbm, d_all.at[ring], local_sem.at[1])
    own_direct = pltpu.make_async_copy(direct_hbm, direct_ref, local_sem.at[2])
    own_direct.start()
    own_e.start()
    own_d.start()

    pl.semaphore_wait(barrier, expected)

    part = span // 4

    def piece(block, index):
        return d_all.at[block, pl.ds(index * part, part)]

    def d_copy(way, step, index, own):
        block = lax.rem(ring + (step if way else -step) + RING, RING)
        src = d_hbm.at[pl.ds(index * part, part)] if own else piece(block, index)
        return pltpu.make_async_remote_copy(
            src_ref=src,
            dst_ref=piece(block, index),
            send_sem=d_send.at[way, step, index],
            recv_sem=d_recv.at[way, step, index],
            device_id=left if way else right,
            device_id_type=MESH,
        )

    def d_arrival(way, step, index):
        block = lax.rem(ring + (step + 1 if way else -step - 1) + RING, RING)
        return pltpu.make_async_remote_copy(
            src_ref=piece(block, index),
            dst_ref=piece(block, index),
            send_sem=d_send.at[way, step, index],
            recv_sem=d_recv.at[way, step, index],
            device_id=left if way else right,
            device_id_type=MESH,
        )

    for index in range(4):
        for way in range(2):
            d_copy(way, 0, index, True).start()
    e_copy = pltpu.make_async_remote_copy(
        src_ref=e_hbm,
        dst_ref=e_all.at[half],
        send_sem=e_send,
        recv_sem=e_recv,
        device_id=mate,
        device_id_type=MESH,
    )
    e_copy.start()

    own_direct.wait()
    for shock in range(2):
        for outp in range(2):
            pad_direct[outp : outp + 1, shock * 64 : shock * 64 + 32] = direct_ref[shock, outp : outp + 1, :]
    raw_direct = pad_direct[...]
    all_direct[0] = jnp.where(core == 0, raw_direct, pltpu.roll(raw_direct, 32, 1))
    direct_copy = pltpu.make_async_remote_copy(
        src_ref=all_direct.at[0],
        dst_ref=all_direct.at[1],
        send_sem=s_send.at[0],
        recv_sem=s_recv.at[0],
        device_id=twin,
        device_id_type=MESH,
    )
    direct_copy.start()

    def swap(turn):
        return pltpu.make_async_remote_copy(
            src_ref=c_buf.at[turn, :, 1 - core],
            dst_ref=x_buf.at[turn],
            send_sem=c_send.at[turn],
            recv_sem=c_recv.at[turn],
            device_id=twin,
            device_id_type=MESH,
        )

    def multiply(block, turn):
        product = lax.dot_general(
            e_all[...].reshape(2 * span, e_all.shape[2]),
            d_all[block],
            (((1,), (1,)), ((), ())),
            preferred_element_type=jnp.float32,
        )
        c_buf[turn] = product.reshape(2, 2, dates, span)
        swap(turn).start()

    def hand_over(block, band_half, turn):
        return pltpu.make_async_remote_copy(
            src_ref=p_buf.at[turn, band_half],
            dst_ref=slots.at[spot],
            send_sem=p_send.at[turn, band_half],
            recv_sem=p_recv.at[spot],
            device_id=owner(block, band_half),
            device_id_type=MESH,
        )

    def to_self(block, band_half):
        return jnp.logical_and(band_half == half, half * RING + block == spot)

    def deliver(block, turn):
        swap(turn).wait_recv()
        p_buf[turn] = c_buf[turn, :, core] + x_buf[turn]
        for band_half in range(2):
            mine = to_self(block, band_half)

            @pl.when(mine)
            def _():
                pltpu.make_async_copy(p_buf.at[turn, band_half], slots.at[spot], p_recv.at[spot]).start()

            @pl.when(jnp.logical_not(mine))
            def _():
                hand_over(block, band_half, turn).start()

    def pass_on(step):
        for index in range(4):
            for way in range(2):
                d_arrival(way, step - 1, index).wait_recv()
                if index // 2 == way:
                    d_copy(way, step, index, False).start()
                else:

                    @pl.when(step < 3)
                    def _():
                        d_copy(way, step, index, False).start()

    def block_at(turn):
        away = (turn + 1) // 2
        return lax.rem(ring + jnp.where(turn % 2 == 1, -away, away) + RING, RING)

    def turn_body(turn, _):
        opens_step = jnp.logical_or(turn == 0, jnp.logical_or(turn == 3, turn == 5))

        @pl.when(opens_step)
        def _():
            pass_on(jnp.where(turn == 0, 1, (turn + 1) // 2))

        @pl.when(turn == 0)
        def _():
            own_e.wait()
            own_d.wait()
            e_copy.wait_recv()

        @pl.when(turn == 7)
        def _():
            for index in range(4):
                d_arrival(index // 2, 3, index).wait_recv()
            for target in [mate] + [x_peer(step) for step in (1, 2, 3)] + [mate_x_peer(step) for step in (1, 2, 3)]:
                pl.semaphore_signal(word_sem.at[0], inc=1, device_id=target, device_id_type=MESH)

        multiply(block_at(turn), turn)

        @pl.when(jnp.logical_and(turn % 2 == 0, turn > 0))
        def _():
            deliver(block_at(turn - 1), turn - 1)

        @pl.when(jnp.logical_or(turn % 2 == 0, turn == 7))
        def _():
            deliver(block_at(turn), turn)

        return 0

    lax.fori_loop(0, RING, turn_body, 0)
    pl.semaphore_wait(word_sem.at[0], 7)
    for step in (1, 2, 3):
        pl.semaphore_signal(word_sem.at[1], inc=1, device_id=y_peer(step), device_id_type=MESH)

    def arrived(index, _):
        pltpu.make_async_copy(slots.at[index], slots.at[index], p_recv.at[index]).wait()
        return 0

    lax.fori_loop(0, SPOTS, arrived, 0)
    total = slots[0]
    for index in range(1, SPOTS):
        total = total + slots[index]

    direct_copy.wait_recv()
    both_direct = all_direct[0] + all_direct[1]
    top = jnp.where(core == 0, both_direct[0:1], both_direct[1:2])
    top = jnp.where(row == 0, top, jnp.zeros_like(top))
    times = lax.broadcasted_iota(jnp.int32, (dates, span), 0)
    lanes = lax.broadcasted_iota(jnp.int32, (dates, span), 1)
    total = total + jnp.where(times == 0, top, 0.0)

    skewed = []
    for shock in range(2):
        tile = total if shock == 0 else pltpu.roll(total, 64, 1)
        tile = jnp.where(lanes < 64, tile, 0.0)
        for bit in range(3):
            moved = pltpu.roll(tile, 1 << bit, 1)
            tile = jnp.where(((63 - times) >> bit) & 1 == 1, moved, tile)
        groups = [tile[start : start + 8] for start in range(0, dates, 8)]
        groups = [
            pltpu.roll(group, dates - 8 - 8 * index, 1) if index < RING - 1 else group
            for index, group in enumerate(groups)
        ]
        tile = jnp.concatenate(groups, axis=0)
        skewed.append(tile)
        ends[shock : shock + 1, :] = jnp.sum(tile, axis=0, keepdims=True)

    def end_copy(down, side):
        valid, target = link(down, side, 1)
        return valid, pltpu.make_async_remote_copy(
            src_ref=ends,
            dst_ref=carry.at[down, side + 1],
            send_sem=n_send.at[down, side + 1],
            recv_sem=n_recv.at[down, side + 1],
            device_id=target,
            device_id_type=MESH,
        )

    def send_ends(near, _):
        for side in (-1, 0, 1):
            valid, copy = end_copy(ROWS - 1 - near, side)

            @pl.when(valid)
            def _():
                copy.start()

        return 0

    pl.semaphore_wait(word_sem.at[1], 3)
    lax.fori_loop(0, ROWS, send_ends, 0)

    summed = []
    for tile in skewed:
        for bit in range(6):
            offset = 1 << bit
            moved = pltpu.roll(tile, offset, 0)
            tile = tile + jnp.where(times >= offset, moved, 0.0)
        summed.append(tile)

    def left_d(step, _):
        for index in range(4):
            for way in range(2):
                if index // 2 == way:
                    d_copy(way, step, index, False).wait_send()
                else:

                    @pl.when(step < 3)
                    def _():
                        d_copy(way, step, index, False).wait_send()

        return 0

    lax.fori_loop(0, 4, left_d, 0)
    e_copy.wait_send()
    direct_copy.wait_send()

    def left_p(turn, _):
        swap(turn).wait_send()
        block = block_at(turn)
        for band_half in range(2):

            @pl.when(jnp.logical_not(to_self(block, band_half)))
            def _():
                hand_over(block, band_half, turn).wait_send()

        return 0

    lax.fori_loop(0, RING, left_p, 0)

    def receive_ends(down, _):
        for side in (-1, 0, 1):
            valid, _u = link(down, side, -1)

            @pl.when(valid)
            def _():
                end_copy(down, side)[1].wait_recv()

        return 0

    lax.fori_loop(0, ROWS, receive_ends, 0)
    incoming = jnp.sum(carry[...], axis=0)
    lane_row = lax.broadcasted_iota(jnp.int32, (2, span), 1)
    before = incoming[1]
    before = before + jnp.where(lane_row < 64, pltpu.roll(incoming[2], 64, 1), 0.0)
    before = before + jnp.where(lane_row >= 64, pltpu.roll(incoming[0], 64, 1), 0.0)

    finished = []
    for shock in range(2):
        tile = summed[shock] + before[shock : shock + 1]
        tile = pltpu.roll(tile, span - 63, 1, stride=1, stride_axis=0)
        finished.append(tile)

    lower = finished
    upper = [pltpu.roll(tile, span - 32, 1) for tile in finished]
    mine = [jnp.where(core == 0, a, b) for a, b in zip(lower, upper)]
    theirs = [jnp.where(core == 0, b, a) for a, b in zip(lower, upper)]
    swap_out[...] = jnp.where(lanes < 32, theirs[0], pltpu.roll(theirs[1], 32, 1))
    last = pltpu.make_async_remote_copy(
        src_ref=swap_out,
        dst_ref=swap_in,
        send_sem=s_send.at[1],
        recv_sem=s_recv.at[1],
        device_id=twin,
        device_id_type=MESH,
    )
    last.start()
    for shock in range(2):
        out_ref[core, shock] = mine[shock][:, :32]

    def left_n(down, _):
        for side in (-1, 0, 1):
            valid, copy = end_copy(down, side)

            @pl.when(valid)
            def _():
                copy.wait_send()

        return 0

    lax.fori_loop(0, ROWS, left_n, 0)
    last.wait()
    received = swap_in[...]
    out_ref[1 - core, 0] = received[:, :32]
    out_ref[1 - core, 1] = pltpu.roll(received, span - 32, 1)[:, :32]


def blocks(expect, distrib, direct):
    outs, dates, points = expect.shape
    span = outs * dates
    dma = pltpu.SemaphoreType.DMA
    return pl.pallas_call(
        kernel,
        out_shape=jax.ShapeDtypeStruct((2, 2, dates, dates // 2), jnp.float32),
        in_specs=[
            pl.BlockSpec(memory_space=pl.ANY),
            pl.BlockSpec(memory_space=pl.ANY),
            pl.BlockSpec(memory_space=pl.ANY),
        ],
        out_specs=pl.BlockSpec(memory_space=pltpu.VMEM),
        scratch_shapes=[
            pltpu.VMEM((PAIR, span, points), jnp.bfloat16),
            pltpu.VMEM((RING, span, points), jnp.bfloat16),
            pltpu.VMEM((RING, PAIR, 2, dates, span), jnp.float32),
            pltpu.VMEM((RING, PAIR, dates, span), jnp.float32),
            pltpu.VMEM((RING, PAIR, dates, span), jnp.float32),
            pltpu.VMEM((SPOTS, dates, span), jnp.float32),
            pltpu.VMEM((2, span), jnp.float32),
            pltpu.VMEM((ROWS, 3, 2, span), jnp.float32),
            pltpu.VMEM((2, 2, dates // 2), jnp.float32),
            pltpu.VMEM((8, span), jnp.float32),
            pltpu.VMEM((2, 8, span), jnp.float32),
            pltpu.VMEM((dates, span), jnp.float32),
            pltpu.VMEM((dates, span), jnp.float32),
            dma((3,)),
            dma,
            dma,
            dma((2, 4, 4)),
            dma((2, 4, 4)),
            dma((RING,)),
            dma((RING,)),
            dma((RING, PAIR)),
            dma((SPOTS,)),
            dma((ROWS, 3)),
            dma((ROWS, 3)),
            dma((2,)),
            dma((2,)),
            pltpu.SemaphoreType.REGULAR((2,)),
        ],
        compiler_params=pltpu.CompilerParams(
            collective_id=0, has_side_effects=True, vmem_limit_bytes=58 * 1024 * 1024
        ),
    )(expect.reshape(span, points), distrib.reshape(span, points), direct)


def shards(expect, distrib, direct, pair_index):
    products = blocks(expect, distrib, direct)
    shock = pair_index[:, 0][:, None, None]
    outp = pair_index[:, 1][:, None, None]
    first = jnp.where(shock == 0, products[0, 0], products[0, 1])
    second = jnp.where(shock == 0, products[1, 0], products[1, 1])
    return jnp.where(outp == 0, first, second)


def solution(mesh):
    placed = (P(None, "hrow", "hcol"), P(None, "hrow", "hcol"), P(None, None, "hcol"), P())
    return jax.shard_map(
        shards, mesh=mesh, in_specs=placed, out_specs=P(None, "hrow", "hcol"), check_vma=False
    )
```

```python
import jax
import jax.numpy as jnp
from jax import lax
from jax.experimental import pallas as pl
from jax.experimental.pallas import tpu as pltpu
from jax.sharding import PartitionSpec as P

PAIR = 2
RING = 8
COLS_X = 4
COLS_Y = 4
CORES = 2
ROWS = PAIR * RING
SPOTS = COLS_X * COLS_Y
MESH = pl.DeviceIdType.MESH


def kernel(
    e_hbm,
    d_hbm,
    direct_hbm,
    out_ref,
    e_all,
    d_all,
    c_buf,
    x_buf,
    p_buf,
    slots,
    ends,
    carry,
    direct_ref,
    pad_direct,
    all_direct,
    swap_out,
    swap_in,
    local_sem,
    e_send,
    e_recv,
    d_send,
    d_recv,
    c_send,
    c_recv,
    p_send,
    p_recv,
    n_send,
    n_recv,
    s_send,
    s_recv,
    word_sem,
):
    row = lax.axis_index("hrow")
    col = lax.axis_index("hcol")
    half = row // RING
    ring = row % RING
    core = col % CORES
    spot = col // CORES
    span = d_hbm.shape[0]
    dates = span // 2

    def ring_id(step):
        return (half * RING + lax.rem(ring + step + RING, RING), col)

    right, left = ring_id(1), ring_id(-1)
    mate = ((1 - half) * RING + ring, col)
    twin = (row, spot * CORES + (1 - core))

    def x_peer(step):
        return (row, lax.rem(spot + COLS_Y * step, SPOTS) * CORES + core)

    def mate_x_peer(step):
        return (mate[0], x_peer(step)[1])

    def y_peer(step):
        return (row, (spot // COLS_Y * COLS_Y + lax.rem(spot + step, COLS_Y)) * CORES + core)

    def owner(block, band_half):
        return (band_half * RING + ring, (half * RING + block) * CORES + core)

    def signal(target):
        pl.semaphore_signal(barrier, inc=1, device_id=target, device_id_type=MESH)


    carry[...] = jnp.zeros_like(carry)
    pad_direct[...] = jnp.zeros_like(pad_direct)

    barrier = pltpu.get_barrier_semaphore()
    for target in (right, left, mate, twin):
        signal(target)
    for step in (1, 2, 3):
        signal(x_peer(step))
        signal(y_peer(step))
        signal(mate_x_peer(step))
    source_half = spot // RING

    def greet_source(index, count):
        same = jnp.logical_and(source_half == half, index == spot)

        @pl.when(jnp.logical_not(same))
        def _():
            signal((source_half * RING + ring, index * CORES + core))

        return count + jnp.where(same, 0, 1)

    expected = lax.fori_loop(0, SPOTS, greet_source, jnp.int32(13))

    def link(down, side, way):
        other_row = row + way * down
        other_spot = spot + way * (down + side)
        valid = jnp.logical_and(other_row >= 0, other_row < ROWS)
        valid = jnp.logical_and(valid, jnp.logical_and(other_spot >= 0, other_spot < SPOTS))
        if side < 1:
            valid = jnp.logical_and(valid, down > 0)
        return valid, (other_row, other_spot * CORES + core)

    own_e = pltpu.make_async_copy(e_hbm, e_all.at[half], local_sem.at[0])
    own_d = pltpu.make_async_copy(d_hbm, d_all.at[ring], local_sem.at[1])
    own_direct = pltpu.make_async_copy(direct_hbm, direct_ref, local_sem.at[2])
    own_direct.start()
    own_e.start()
    own_d.start()

    pl.semaphore_wait(barrier, expected)

    part = span // 4

    def piece(block, index):
        return d_all.at[block, pl.ds(index * part, part)]

    def d_copy(way, step, index, own):
        block = lax.rem(ring + (step if way else -step) + RING, RING)
        src = d_hbm.at[pl.ds(index * part, part)] if own else piece(block, index)
        return pltpu.make_async_remote_copy(
            src_ref=src,
            dst_ref=piece(block, index),
            send_sem=d_send.at[way, step, index],
            recv_sem=d_recv.at[way, step, index],
            device_id=left if way else right,
            device_id_type=MESH,
        )

    def d_arrival(way, step, index):
        block = lax.rem(ring + (step + 1 if way else -step - 1) + RING, RING)
        return pltpu.make_async_remote_copy(
            src_ref=piece(block, index),
            dst_ref=piece(block, index),
            send_sem=d_send.at[way, step, index],
            recv_sem=d_recv.at[way, step, index],
            device_id=left if way else right,
            device_id_type=MESH,
        )

    for index in range(4):
        for way in range(2):
            d_copy(way, 0, index, True).start()
    e_copy = pltpu.make_async_remote_copy(
        src_ref=e_hbm,
        dst_ref=e_all.at[half],
        send_sem=e_send,
        recv_sem=e_recv,
        device_id=mate,
        device_id_type=MESH,
    )
    e_copy.start()

    own_direct.wait()
    for shock in range(2):
        for outp in range(2):
            pad_direct[outp : outp + 1, shock * 64 : shock * 64 + 32] = direct_ref[shock, outp : outp + 1, :]
    raw_direct = pad_direct[...]
    all_direct[0] = jnp.where(core == 0, raw_direct, pltpu.roll(raw_direct, 32, 1))
    direct_copy = pltpu.make_async_remote_copy(
        src_ref=all_direct.at[0],
        dst_ref=all_direct.at[1],
        send_sem=s_send.at[0],
        recv_sem=s_recv.at[0],
        device_id=twin,
        device_id_type=MESH,
    )
    direct_copy.start()

    def swap(turn):
        return pltpu.make_async_remote_copy(
            src_ref=c_buf.at[turn, :, 1 - core],
            dst_ref=x_buf.at[turn],
            send_sem=c_send.at[turn],
            recv_sem=c_recv.at[turn],
            device_id=twin,
            device_id_type=MESH,
        )

    def multiply(block, turn):
        for outp in (1 - core, core):
            rows = e_all[:, pl.ds(pl.multiple_of(outp * dates, dates), dates)]
            product = lax.dot_general(
                rows.reshape(span, e_all.shape[2]),
                d_all[block],
                (((1,), (1,)), ((), ())),
                preferred_element_type=jnp.float32,
            )
            c_buf[turn, :, outp] = product.reshape(2, dates, span)
            if outp is not core:
                swap(turn).start()

    def hand_over(block, band_half, turn):
        return pltpu.make_async_remote_copy(
            src_ref=p_buf.at[turn, band_half],
            dst_ref=slots.at[spot],
            send_sem=p_send.at[turn, band_half],
            recv_sem=p_recv.at[spot],
            device_id=owner(block, band_half),
            device_id_type=MESH,
        )

    def to_self(block, band_half):
        return jnp.logical_and(band_half == half, half * RING + block == spot)

    def deliver(block, turn):
        swap(turn).wait_recv()
        p_buf[turn] = c_buf[turn, :, core] + x_buf[turn]
        for band_half in range(2):
            mine = to_self(block, band_half)

            @pl.when(mine)
            def _():
                pltpu.make_async_copy(p_buf.at[turn, band_half], slots.at[spot], p_recv.at[spot]).start()

            @pl.when(jnp.logical_not(mine))
            def _():
                hand_over(block, band_half, turn).start()

    def pass_on(step):
        for index in range(4):
            for way in range(2):
                d_arrival(way, step - 1, index).wait_recv()
                if index // 2 == way:
                    d_copy(way, step, index, False).start()
                else:

                    @pl.when(step < 3)
                    def _():
                        d_copy(way, step, index, False).start()

    def block_at(turn):
        away = (turn + 1) // 2
        return lax.rem(ring + jnp.where(turn % 2 == 1, -away, away) + RING, RING)

    def turn_body(turn, _):
        opens_step = jnp.logical_or(turn == 0, jnp.logical_or(turn == 3, turn == 5))

        @pl.when(opens_step)
        def _():
            pass_on(jnp.where(turn == 0, 1, (turn + 1) // 2))

        @pl.when(turn == 0)
        def _():
            own_e.wait()
            own_d.wait()
            e_copy.wait_recv()

        @pl.when(turn == 7)
        def _():
            for index in range(4):
                d_arrival(index // 2, 3, index).wait_recv()
            for target in [mate] + [x_peer(step) for step in (1, 2, 3)] + [mate_x_peer(step) for step in (1, 2, 3)]:
                pl.semaphore_signal(word_sem.at[0], inc=1, device_id=target, device_id_type=MESH)

        multiply(block_at(turn), turn)

        @pl.when(jnp.logical_and(turn % 2 == 0, turn > 0))
        def _():
            deliver(block_at(turn - 1), turn - 1)

        @pl.when(jnp.logical_or(turn % 2 == 0, turn == 7))
        def _():
            deliver(block_at(turn), turn)

        return 0

    lax.fori_loop(0, RING, turn_body, 0)
    pl.semaphore_wait(word_sem.at[0], 7)
    for step in (1, 2, 3):
        pl.semaphore_signal(word_sem.at[1], inc=1, device_id=y_peer(step), device_id_type=MESH)

    def arrived(index, _):
        pltpu.make_async_copy(slots.at[index], slots.at[index], p_recv.at[index]).wait()
        return 0

    lax.fori_loop(0, SPOTS, arrived, 0)
    total = slots[0]
    for index in range(1, SPOTS):
        total = total + slots[index]

    direct_copy.wait_recv()
    both_direct = all_direct[0] + all_direct[1]
    top = jnp.where(core == 0, both_direct[0:1], both_direct[1:2])
    top = jnp.where(row == 0, top, jnp.zeros_like(top))
    times = lax.broadcasted_iota(jnp.int32, (dates, span), 0)
    lanes = lax.broadcasted_iota(jnp.int32, (dates, span), 1)
    total = total + jnp.where(times == 0, top, 0.0)

    skewed = []
    for shock in range(2):
        tile = total if shock == 0 else pltpu.roll(total, 64, 1)
        tile = jnp.where(lanes < 64, tile, 0.0)
        for bit in range(3):
            moved = pltpu.roll(tile, 1 << bit, 1)
            tile = jnp.where(((63 - times) >> bit) & 1 == 1, moved, tile)
        groups = [tile[start : start + 8] for start in range(0, dates, 8)]
        groups = [
            pltpu.roll(group, dates - 8 - 8 * index, 1) if index < RING - 1 else group
            for index, group in enumerate(groups)
        ]
        tile = jnp.concatenate(groups, axis=0)
        skewed.append(tile)
        ends[shock : shock + 1, :] = jnp.sum(tile, axis=0, keepdims=True)

    def end_copy(down, side):
        valid, target = link(down, side, 1)
        return valid, pltpu.make_async_remote_copy(
            src_ref=ends,
            dst_ref=carry.at[down, side + 1],
            send_sem=n_send.at[down, side + 1],
            recv_sem=n_recv.at[down, side + 1],
            device_id=target,
            device_id_type=MESH,
        )

    def send_ends(near, _):
        for side in (-1, 0, 1):
            valid, copy = end_copy(ROWS - 1 - near, side)

            @pl.when(valid)
            def _():
                copy.start()

        return 0

    pl.semaphore_wait(word_sem.at[1], 3)
    lax.fori_loop(0, ROWS, send_ends, 0)

    summed = []
    for tile in skewed:
        for bit in range(6):
            offset = 1 << bit
            moved = pltpu.roll(tile, offset, 0)
            tile = tile + jnp.where(times >= offset, moved, 0.0)
        summed.append(tile)

    def left_d(step, _):
        for index in range(4):
            for way in range(2):
                if index // 2 == way:
                    d_copy(way, step, index, False).wait_send()
                else:

                    @pl.when(step < 3)
                    def _():
                        d_copy(way, step, index, False).wait_send()

        return 0

    lax.fori_loop(0, 4, left_d, 0)
    e_copy.wait_send()
    direct_copy.wait_send()

    def left_p(turn, _):
        swap(turn).wait_send()
        block = block_at(turn)
        for band_half in range(2):

            @pl.when(jnp.logical_not(to_self(block, band_half)))
            def _():
                hand_over(block, band_half, turn).wait_send()

        return 0

    lax.fori_loop(0, RING, left_p, 0)

    def receive_ends(down, _):
        for side in (-1, 0, 1):
            valid, _u = link(down, side, -1)

            @pl.when(valid)
            def _():
                end_copy(down, side)[1].wait_recv()

        return 0

    lax.fori_loop(0, ROWS, receive_ends, 0)
    incoming = jnp.sum(carry[...], axis=0)
    lane_row = lax.broadcasted_iota(jnp.int32, (2, span), 1)
    before = incoming[1]
    before = before + jnp.where(lane_row < 64, pltpu.roll(incoming[2], 64, 1), 0.0)
    before = before + jnp.where(lane_row >= 64, pltpu.roll(incoming[0], 64, 1), 0.0)

    finished = []
    for shock in range(2):
        tile = summed[shock] + before[shock : shock + 1]
        tile = pltpu.roll(tile, span - 63, 1, stride=1, stride_axis=0)
        finished.append(tile)

    lower = finished
    upper = [pltpu.roll(tile, span - 32, 1) for tile in finished]
    mine = [jnp.where(core == 0, a, b) for a, b in zip(lower, upper)]
    theirs = [jnp.where(core == 0, b, a) for a, b in zip(lower, upper)]
    swap_out[...] = jnp.where(lanes < 32, theirs[0], pltpu.roll(theirs[1], 32, 1))
    last = pltpu.make_async_remote_copy(
        src_ref=swap_out,
        dst_ref=swap_in,
        send_sem=s_send.at[1],
        recv_sem=s_recv.at[1],
        device_id=twin,
        device_id_type=MESH,
    )
    last.start()
    for shock in range(2):
        out_ref[core, shock] = mine[shock][:, :32]

    def left_n(down, _):
        for side in (-1, 0, 1):
            valid, copy = end_copy(down, side)

            @pl.when(valid)
            def _():
                copy.wait_send()

        return 0

    lax.fori_loop(0, ROWS, left_n, 0)
    last.wait()
    received = swap_in[...]
    out_ref[1 - core, 0] = received[:, :32]
    out_ref[1 - core, 1] = pltpu.roll(received, span - 32, 1)[:, :32]


def blocks(expect, distrib, direct):
    outs, dates, points = expect.shape
    span = outs * dates
    dma = pltpu.SemaphoreType.DMA
    return pl.pallas_call(
        kernel,
        out_shape=jax.ShapeDtypeStruct((2, 2, dates, dates // 2), jnp.float32),
        in_specs=[
            pl.BlockSpec(memory_space=pl.ANY),
            pl.BlockSpec(memory_space=pl.ANY),
            pl.BlockSpec(memory_space=pl.ANY),
        ],
        out_specs=pl.BlockSpec(memory_space=pltpu.VMEM),
        scratch_shapes=[
            pltpu.VMEM((PAIR, span, points), jnp.bfloat16),
            pltpu.VMEM((RING, span, points), jnp.bfloat16),
            pltpu.VMEM((RING, PAIR, 2, dates, span), jnp.float32),
            pltpu.VMEM((RING, PAIR, dates, span), jnp.float32),
            pltpu.VMEM((RING, PAIR, dates, span), jnp.float32),
            pltpu.VMEM((SPOTS, dates, span), jnp.float32),
            pltpu.VMEM((2, span), jnp.float32),
            pltpu.VMEM((ROWS, 3, 2, span), jnp.float32),
            pltpu.VMEM((2, 2, dates // 2), jnp.float32),
            pltpu.VMEM((8, span), jnp.float32),
            pltpu.VMEM((2, 8, span), jnp.float32),
            pltpu.VMEM((dates, span), jnp.float32),
            pltpu.VMEM((dates, span), jnp.float32),
            dma((3,)),
            dma,
            dma,
            dma((2, 4, 4)),
            dma((2, 4, 4)),
            dma((RING,)),
            dma((RING,)),
            dma((RING, PAIR)),
            dma((SPOTS,)),
            dma((ROWS, 3)),
            dma((ROWS, 3)),
            dma((2,)),
            dma((2,)),
            pltpu.SemaphoreType.REGULAR((2,)),
        ],
        compiler_params=pltpu.CompilerParams(
            collective_id=0, has_side_effects=True, vmem_limit_bytes=58 * 1024 * 1024
        ),
    )(expect.reshape(span, points), distrib.reshape(span, points), direct)


def shards(expect, distrib, direct, pair_index):
    products = blocks(expect, distrib, direct)
    shock = pair_index[:, 0][:, None, None]
    outp = pair_index[:, 1][:, None, None]
    first = jnp.where(shock == 0, products[0, 0], products[0, 1])
    second = jnp.where(shock == 0, products[1, 0], products[1, 1])
    return jnp.where(outp == 0, first, second)


def solution(mesh):
    placed = (P(None, "hrow", "hcol"), P(None, "hrow", "hcol"), P(None, None, "hcol"), P())
    return jax.shard_map(
        shards, mesh=mesh, in_specs=placed, out_specs=P(None, "hrow", "hcol"), check_vma=False
    )
```
